32 devices in a mesh: grp: 4 (over y, x), dev: 8 (over z, core).
Axes of the slice: x: 2, y: 2, z: 4, core: 2. Of those that a mesh axis runs over, the one named last changes fastest.
Arguments:
- jacobian_blocks: bfloat16 [2048, 3, 128, 128], P(('grp', 'dev'))
- probe_blocks: bfloat16 [2048, 64, 128], P(('grp', 'dev'))
- column_slots: int32 [2048, 2], P(('grp', 'dev')), may hold values from 0 to 127, as said below
- want_inner: int32 [32, 8, 8], P(('grp', 'dev')), may hold values from 0 to 63
- want_outer: int32 [32, 4, 16], P(('grp', 'dev')), may hold values from 0 to 63
Outputs:
- triangle: float32 [64, 64], replicated
- basis_blocks: float32 [2048, 64, 128], P(('grp', 'dev'))
The draws below stay inside these ranges and needn't reach their ends.
Inputs may be any that keep to these rules, and one draw needn't show every extreme that they name: `column_slots`: on every device, the 128 entries of its 64 block rows name each position of that device's remote pool exactly once.
All inputs are finite; a program needn't handle non-finite values.
Results may differ from the reference program's by a relative error of at most 0.0003.
Values may be sent and summed in bfloat16 or wider, within the bound.
No kernel may reach another device: no remote copies, remote signals or barrier semaphores. Data moves between devices by JAX's collectives and lax.ppermute only.
A program may use at most 64 MiB of HBM per device.

```python
import math
import jax
import jax.numpy as jnp
from jax import lax

BLOCK = 128
PROBES = 64
ROW_BLOCKS = 3
RB_DEV = 64
NB_ROWS = 2048
IN_SLOTS = 8
CROSS_SLOTS = 16
N_GRP = 4
N_DEV = 8


def draw_jacobian_blocks(key, part):
    noise_key, scale_key = jax.random.split(key)
    shape_all = (NB_ROWS, ROW_BLOCKS, BLOCK, BLOCK)
    entries = jax.random.normal(noise_key, shape_all, jnp.float32)
    row_scale = jnp.exp(jax.random.uniform(scale_key, (NB_ROWS,), jnp.float32, math.log(0.3), math.log(3.0)))
    ramp = jnp.sqrt(1.0 + 2.0 * jnp.arange(NB_ROWS, dtype=jnp.float32) / NB_ROWS)
    factor = row_scale * ramp * (ROW_BLOCKS * BLOCK) ** (-0.5)
    return (entries * factor[:, None, None, None]).astype(jnp.bfloat16)


def draw_probe_blocks(key, part):
    noise_key, scale_key, common_key, load_key = jax.random.split(key, 4)
    shape_all = (NB_ROWS, PROBES, BLOCK)
    shared_count = 4
    common = jax.random.normal(common_key, (shared_count, NB_ROWS, BLOCK), jnp.float32)
    entries = jax.random.normal(noise_key, shape_all, jnp.float32)
    loadings = 0.7 * jax.random.normal(load_key, (shared_count, PROBES), jnp.float32)
    mixed = entries
    for shared_index in range(shared_count):
        mixed = mixed + loadings[shared_index][None, :, None] * common[shared_index][:, None, :]
    column_scale = jnp.exp(jax.random.uniform(scale_key, (PROBES,), jnp.float32, math.log(0.5), math.log(2.0)))
    return (mixed * column_scale[None, :, None]).astype(jnp.bfloat16)


def draw_column_slots(key, part):
    device_keys = jax.random.split(key, NB_ROWS // RB_DEV)

    def shuffled(device_key):
        return jax.random.permutation(device_key, 2 * RB_DEV)
    orders = jax.vmap(shuffled)(device_keys)
    return orders.reshape(NB_ROWS, 2).astype(jnp.int32)


def set_ends(result, key, low, high):
    place = [jax.random.randint(jax.random.fold_in(key, axis), (), 0, length) for axis, length in enumerate(result.shape)]
    main_axis = result.shape.index(max(result.shape))
    neighbour = place[:main_axis] + [(place[main_axis] + 1) % result.shape[main_axis]] + place[main_axis + 1:]
    return result.at[tuple(place)].set(low).at[tuple(neighbour)].set(high)


def setup_inputs(seed: int = 0) -> dict:
    streams_of = jax.random.split(jax.random.key(seed), 6)
    jacobian_blocks = draw_jacobian_blocks(jax.random.fold_in(streams_of[5], 71), 0)
    probe_blocks = draw_probe_blocks(jax.random.fold_in(streams_of[5], 71), 0)
    column_slots = draw_column_slots(jax.random.fold_in(streams_of[5], 71), 0)
    want_inner = set_ends(jax.random.randint(streams_of[3], (RB_DEV * 0 + N_GRP * N_DEV, N_DEV, IN_SLOTS), 0, RB_DEV), jax.random.fold_in(streams_of[3], 1), 0, RB_DEV - 1).astype(jnp.int32)
    want_outer = set_ends(jax.random.randint(streams_of[4], (N_GRP * N_DEV, N_GRP, CROSS_SLOTS), 0, RB_DEV), jax.random.fold_in(streams_of[4], 1), 0, RB_DEV - 1).astype(jnp.int32)
    return {"jacobian_blocks": jacobian_blocks, "probe_blocks": probe_blocks, "column_slots": column_slots, "want_inner": want_inner, "want_outer": want_outer}


exact_precision = lax.Precision.HIGHEST

def device_sketch(device_number, jacobian_blocks, probe_blocks, column_slots, want_inner, want_outer):
    group_id = device_number // N_DEV
    within = device_number % N_DEV
    first_row = device_number * RB_DEV
    own_probe = lax.dynamic_slice_in_dim(probe_blocks, first_row, RB_DEV, 0).astype(jnp.float32)
    own_rows = lax.dynamic_slice_in_dim(jacobian_blocks, first_row, RB_DEV, 0).astype(jnp.float32)
    slot_pairs = lax.dynamic_slice_in_dim(column_slots, first_row, RB_DEV, 0)
    inner_wants = lax.dynamic_index_in_dim(want_inner, device_number, 0, keepdims=False)
    outer_wants = lax.dynamic_index_in_dim(want_outer, device_number, 0, keepdims=False)
    inner_rows = ((group_id * N_DEV + jnp.arange(N_DEV, dtype=jnp.int32)) * RB_DEV)[:, None] + inner_wants
    outer_rows = ((jnp.arange(N_GRP, dtype=jnp.int32) * N_DEV + within) * RB_DEV)[:, None] + outer_wants
    remote = jnp.concatenate([jnp.take(probe_blocks, inner_rows.reshape(-1), axis=0), jnp.take(probe_blocks, outer_rows.reshape(-1), axis=0)], 0).astype(jnp.float32)
    near_probe = jnp.take(remote, slot_pairs[:, 0], axis=0)
    other_probe = jnp.take(remote, slot_pairs[:, 1], axis=0)
    sketch = jnp.einsum('rpc,rac->rpa', own_probe, own_rows[:, 0], precision=exact_precision)
    sketch = sketch + jnp.einsum('rpc,rac->rpa', near_probe, own_rows[:, 1], precision=exact_precision)
    sketch = sketch + jnp.einsum('rpc,rac->rpa', other_probe, own_rows[:, 2], precision=exact_precision)
    gram_part = jnp.einsum('rpa,rqa->pq', sketch, sketch, precision=exact_precision)
    return (sketch, gram_part)

def reference(jacobian_blocks, probe_blocks, column_slots, want_inner, want_outer):

    def one_device(device_number):
        return device_sketch(device_number, jacobian_blocks, probe_blocks, column_slots, want_inner, want_outer)
    sketches, grams = lax.map(one_device, jnp.arange(N_GRP * N_DEV, dtype=jnp.int32))
    sketch = sketches.reshape(NB_ROWS, PROBES, BLOCK)
    gram = jnp.sum(grams, axis=0) / jnp.float32(NB_ROWS * BLOCK)
    lower = jnp.linalg.cholesky(gram)
    inverse = jax.scipy.linalg.solve_triangular(lower, jnp.eye(PROBES, dtype=jnp.float32), lower=True)
    basis_blocks = jnp.einsum('pq,rqa->rpa', inverse, sketch, precision=exact_precision)
    return (lower.T, basis_blocks)
```

```python
import functools

import jax
import jax.numpy as jnp
from jax import lax
from jax.experimental import pallas as pl
from jax.experimental.pallas import tpu as pltpu
from jax.sharding import PartitionSpec as P

exact_precision = lax.Precision.HIGHEST
NT = (((1,), (1,)), ((), ()))


def swapped(shard, axis, mask):
    return lax.ppermute(shard, axis, [(i, i ^ mask) for i in range(lax.axis_size(axis))])


def masks_of(size):
    return sorted(range(1, size), reverse=True)


def asked(wants, axis):
    masks = masks_of(lax.axis_size(axis))
    if len(masks) < 8:
        return [swapped(wants, axis, m) for m in masks] + [wants]
    return [lax.all_to_all(wants, axis, split_axis=0, concat_axis=0, tiled=True)]


def gather_kernel(sources, counts, *refs):
    place = refs[0]
    asks = refs[1 : 1 + counts]
    probe = refs[1 + counts]
    outs = refs[2 + counts :]
    for (mine, source, mask), out in zip(sources, outs):
        row = place[mine] if mask is None else place[mine] ^ mask
        for c in range(out.shape[0]):
            out[c] = probe[asks[source][row, c]]


def gathered(place, all_asks, all_masks, probe_blocks):
    block = probe_blocks.shape[1:]
    flat, sources, shapes = [], [], []
    for mine, (asks, masks) in enumerate(zip(all_asks, all_masks)):
        direct = len(asks) == len(masks)
        for n, mask in enumerate(masks):
            sources.append((mine, len(flat) + (n if direct else 0), None if direct else mask))
            shapes.append(
                jax.ShapeDtypeStruct((asks[0].shape[1],) + block, probe_blocks.dtype)
            )
        flat += asks
    total = sum(s.size for s in shapes) * 2
    return pl.pallas_call(
        functools.partial(gather_kernel, sources, len(flat)),
        out_shape=shapes,
        in_specs=[pl.BlockSpec(memory_space=pltpu.SMEM)] * (1 + len(flat))
        + [pl.BlockSpec(memory_space=pltpu.VMEM)],
        out_specs=[pl.BlockSpec(memory_space=pltpu.VMEM)] * len(shapes),
        cost_estimate=pl.CostEstimate(flops=0, bytes_accessed=2 * total, transcendentals=0),
        name="gather",
    )(place, *flat, probe_blocks)


def diagonal_kernel(probe, jac, out):
    for r in range(out.shape[0]):
        out[r] = lax.dot_general(probe[r], jac[r, 0], NT, preferred_element_type=jnp.float32)


def diagonal_part(probe_blocks, jacobian_blocks, step_rows):
    rows, probes, block = probe_blocks.shape
    return pl.pallas_call(
        diagonal_kernel,
        grid=(rows // step_rows,),
        out_shape=jax.ShapeDtypeStruct(probe_blocks.shape, jnp.float32),
        in_specs=[
            pl.BlockSpec((step_rows, probes, block), lambda s: (s, 0, 0)),
            pl.BlockSpec((step_rows, 1, block, block), lambda s: (s, 0, 0, 0)),
        ],
        out_specs=pl.BlockSpec((step_rows, probes, block), lambda s: (s, 0, 0)),
        cost_estimate=pl.CostEstimate(
            flops=2 * rows * probes * block * block,
            bytes_accessed=rows * (probes * block * 6 + block * block * 2),
            transcendentals=0,
        ),
        name="diagonal",
    )(probe_blocks, jacobian_blocks)


def sketch_kernel(inner_count, outer_count, step_rows, steps, *refs):
    place, slots = refs[:2]
    inner = refs[2 : 2 + inner_count]
    outer = refs[2 + inner_count : 2 + inner_count + outer_count]
    base, jac1, jac2, sketch, gram, pool, sems, acc = refs[2 + inner_count + outer_count :]
    step = pl.program_id(0)
    inner_slots = inner[0].shape[0]
    outer_slots = outer[0].shape[0]

    @pl.when(step == 0)
    def _():
        copies = []
        for m, buf in enumerate(inner):
            at = (place[0] ^ m) * inner_slots
            copies.append((buf, pool.at[pl.ds(at, inner_slots)]))
        for m, buf in enumerate(outer):
            at = inner_count * inner_slots + (place[1] ^ m) * outer_slots
            copies.append((buf, pool.at[pl.ds(at, outer_slots)]))
        copies = [pltpu.make_async_copy(a, b, sems.at[n]) for n, (a, b) in enumerate(copies)]
        for copy in copies:
            copy.start()
        for copy in copies:
            copy.wait()
        acc[...] = jnp.zeros_like(acc)

    probes = sketch.shape[1]
    for r in range(step_rows):
        row = step * step_rows + r
        one = pool[slots[row, 0]]
        two = pool[slots[row, 1]]
        total = base[r] + lax.dot_general(one, jac1[r, 0], NT, preferred_element_type=jnp.float32)
        total = total + lax.dot_general(two, jac2[r, 0], NT, preferred_element_type=jnp.float32)
        sketch[r] = total
        high = total.astype(jnp.bfloat16)
        low = (total - high.astype(jnp.float32)).astype(jnp.bfloat16)
        both = jnp.concatenate([high, low], 0)
        acc[...] += lax.dot_general(both, high, NT, preferred_element_type=jnp.float32)

    @pl.when(step == steps - 1)
    def _():
        cross = acc[probes:, :]
        gram[...] = acc[:probes, :] + cross + cross.T


def sketched(place, slots, inner, outer, base, jacobian_blocks, step_rows):
    rows, probes, block = base.shape
    steps = rows // step_rows
    pool_size = sum(b.shape[0] for b in inner) + sum(b.shape[0] for b in outer)
    return pl.pallas_call(
        functools.partial(sketch_kernel, len(inner), len(outer), step_rows, steps),
        grid=(steps,),
        out_shape=[
            jax.ShapeDtypeStruct(base.shape, jnp.float32),
            jax.ShapeDtypeStruct((probes, probes), jnp.float32),
        ],
        in_specs=[pl.BlockSpec(memory_space=pltpu.SMEM)] * 2
        + [pl.BlockSpec(memory_space=pl.ANY)] * (len(inner) + len(outer))
        + [
            pl.BlockSpec((step_rows, probes, block), lambda s: (s, 0, 0)),
            pl.BlockSpec((step_rows, 1, block, block), lambda s: (s, 1, 0, 0)),
            pl.BlockSpec((step_rows, 1, block, block), lambda s: (s, 2, 0, 0)),
        ],
        out_specs=[
            pl.BlockSpec((step_rows, probes, block), lambda s: (s, 0, 0)),
            pl.BlockSpec((probes, probes), lambda s: (0, 0)),
        ],
        scratch_shapes=[
            pltpu.VMEM((pool_size, probes, block), jnp.bfloat16),
            pltpu.SemaphoreType.DMA((len(inner) + len(outer),)),
            pltpu.VMEM((2 * probes, probes), jnp.float32),
        ],
        cost_estimate=pl.CostEstimate(
            flops=8 * rows * probes * block * block,
            bytes_accessed=rows * (probes * block * 12 + block * block * 4),
            transcendentals=0,
        ),
        name="sketch",
    )(place, slots, *inner, *outer, base, jacobian_blocks, jacobian_blocks)


def axis_sum(part, axis):
    bits = lax.axis_size(axis).bit_length() - 1
    done = 0
    while done < bits:
        take = min(3, bits - done)
        parts = [part] + [swapped(part, axis, m << done) for m in range(1, 1 << take)]
        part = functools.reduce(jnp.add, parts)
        done += take
    return part


def shards(jacobian_blocks, probe_blocks, column_slots, want_inner, want_outer):
    row_count = jacobian_blocks.shape[0]
    block_size = jacobian_blocks.shape[2]
    probe_count = probe_blocks.shape[1]
    inner_size = lax.axis_size("dev")
    outer_size = lax.axis_size("grp")
    total_rows = row_count * block_size * inner_size * outer_size
    place = jnp.stack([lax.axis_index("dev"), lax.axis_index("grp")]).astype(jnp.int32)
    inner_masks = masks_of(inner_size)
    outer_masks = masks_of(outer_size)
    served = gathered(
        place,
        (asked(want_inner[0], "dev"), asked(want_outer[0], "grp")),
        (inner_masks + [0], outer_masks + [0]),
        probe_blocks,
    )
    inner_served, outer_served = served[:inner_size], served[inner_size:]
    inner = {m: swapped(b, "dev", m) for m, b in zip(inner_masks, inner_served)}
    outer = {m: swapped(b, "grp", m) for m, b in zip(outer_masks, outer_served)}
    inner[0] = inner_served[-1]
    outer[0] = outer_served[-1]
    base = diagonal_part(probe_blocks, jacobian_blocks, 8)
    sketch, gram_part = sketched(
        place,
        column_slots,
        [inner[m] for m in range(inner_size)],
        [outer[m] for m in range(outer_size)],
        base,
        jacobian_blocks,
        8,
    )
    gram = axis_sum(axis_sum(gram_part, "dev"), "grp") / jnp.float32(total_rows)
    lower = jnp.linalg.cholesky(gram)
    inverse = jax.scipy.linalg.solve_triangular(
        lower, jnp.eye(probe_count, dtype=jnp.float32), lower=True
    )
    basis_blocks = jnp.einsum("pq,rqa->rpa", inverse, sketch, precision=exact_precision)
    return (lower.T, basis_blocks)


def solution(mesh):
    return jax.shard_map(
        shards,
        mesh=mesh,
        in_specs=(
            P(("grp", "dev"), None, None, None),
            P(("grp", "dev"), None, None),
            P(("grp", "dev"), None),
            P(("grp", "dev"), None, None),
            P(("grp", "dev"), None, None),
        ),
        out_specs=(P(), P(("grp", "dev"), None, None)),
        check_vma=False,
    )
```

```python
import functools

import jax
import jax.numpy as jnp
from jax import lax
from jax.experimental import pallas as pl
from jax.experimental.pallas import tpu as pltpu
from jax.sharding import PartitionSpec as P

BOTH = ("grp", "dev")
NT = (((1,), (1,)), ((), ()))
NN = (((1,), (0,)), ((), ()))
VMEM = pltpu.VMEM
SMEM = pltpu.SMEM
BF16 = jnp.bfloat16
F32 = jnp.float32
LIMIT = pltpu.CompilerParams(vmem_limit_bytes=24 << 20)


def swapped(shard, axis, mask):
    return lax.ppermute(shard, axis, [(i, i ^ mask) for i in range(lax.axis_size(axis))])


def split_step(shard, even_mask, odd_mask):
    size = lax.axis_size("grp") * lax.axis_size("dev")
    pairs = [(i, i ^ (odd_mask if i & 1 else even_mask)) for i in range(size)]
    return lax.ppermute(shard, BOTH, pairs)


def paired_asks(want_inner, want_outer):
    inner_size = lax.axis_size("dev")
    outer_bits = lax.axis_size("grp").bit_length() - 1
    core = lax.axis_index("dev") & 1
    mine = jnp.concatenate([want_inner.reshape(1, -1), want_outer.reshape(1, -1)], 1)
    twin = swapped(mine, "dev", 1)
    pair = jnp.where(core == 0, jnp.concatenate([mine, twin], 0), jnp.concatenate([twin, mine], 0))
    known = [pair]
    for bit in range(outer_bits):
        known.append(split_step(jnp.concatenate(known, 0), 2 << bit, inner_size << bit))
    far = jnp.concatenate(known[1:], 0)
    return jnp.concatenate([pair, far, swapped(far, "dev", 1)], 0)


def gather_kernel(paired, inner_slots, outer_slots, inner_masks, outer_masks, *refs):
    place = refs[0]
    probe_at = 2 if paired else 3
    probe = refs[probe_at]
    outs = refs[probe_at + 1 :]
    me, group = place[0], place[1]
    core = me & 1
    inner_size, outer_size = len(inner_masks), len(outer_masks)
    far_rows = 2 * outer_size - 2
    inner_base = 2 + core * far_rows - 2
    outer_base = 2 + (1 - core) * far_rows - 2
    for n, mask in enumerate(inner_masks + outer_masks):
        inner = n < inner_size
        out = outs[n]
        if paired:
            if inner:
                row = (core ^ (mask & 1)) + (inner_base + (mask >> 1) * 2 if mask > 1 else 0)
                entry = me * inner_slots
            else:
                row = core + (outer_base + mask * 2 if mask else 0)
                entry = inner_size * inner_slots + group * outer_slots
            for c in range(out.shape[0]):
                out[c] = probe[refs[1][row, entry + c]]
        else:
            row = (me if inner else group) ^ mask
            for c in range(out.shape[0]):
                out[c] = probe[refs[1 if inner else 2][row, c]]


def gathered(place, asks, inner_slots, outer_slots, inner_masks, outer_masks, probe_blocks):
    block = probe_blocks.shape[1:]
    shapes = [VMEM((inner_slots,) + block, BF16)] * len(inner_masks)
    shapes += [VMEM((outer_slots,) + block, BF16)] * len(outer_masks)
    shapes = [jax.ShapeDtypeStruct(s.shape, BF16) for s in shapes]
    total = sum(s.size for s in shapes) * 2
    return pl.pallas_call(
        functools.partial(
            gather_kernel, len(asks) == 1, inner_slots, outer_slots, inner_masks, outer_masks
        ),
        out_shape=shapes,
        in_specs=[pl.BlockSpec(memory_space=SMEM)] * (1 + len(asks))
        + [pl.BlockSpec(memory_space=VMEM)],
        out_specs=[pl.BlockSpec(memory_space=VMEM)] * len(shapes),
        cost_estimate=pl.CostEstimate(flops=0, bytes_accessed=2 * total, transcendentals=0),
        compiler_params=LIMIT,
        name="gather",
    )(place, *asks, probe_blocks)


def early_kernel(chunk, slots, probe, jac, base, flipped, users, jbuf, sems):
    rows = base.shape[0]
    copies = []
    for q in range(rows // chunk):
        part = pl.ds(q * chunk, chunk)
        copies.append(pltpu.make_async_copy(jac.at[part], jbuf.at[part], sems.at[q]))
        copies[-1].start()

    def name_user(r, carry):
        users[slots[r, 0]] = 2 * r
        users[slots[r, 1]] = 2 * r + 1
        return carry

    lax.fori_loop(0, rows, name_user, 0)

    def one_row(r, carry):
        base[r] = lax.dot_general(probe[r], jbuf[r, 0], NT, preferred_element_type=F32)
        flipped[2 * r] = jbuf[r, 1].T
        flipped[2 * r + 1] = jbuf[r, 2].T
        return carry

    for q, copy in enumerate(copies):
        copy.wait()
        lax.fori_loop(q * chunk, (q + 1) * chunk, one_row, 0, unroll=4)


def early_part(slots, probe_blocks, jacobian_blocks, chunk):
    rows, probes, block = probe_blocks.shape
    return pl.pallas_call(
        functools.partial(early_kernel, chunk),
        out_shape=[
            jax.ShapeDtypeStruct(probe_blocks.shape, F32),
            jax.ShapeDtypeStruct((2 * rows, block, block), BF16),
            jax.ShapeDtypeStruct((2 * rows,), jnp.int32),
        ],
        in_specs=[
            pl.BlockSpec(memory_space=SMEM),
            pl.BlockSpec(memory_space=VMEM),
            pl.BlockSpec(memory_space=pl.ANY),
        ],
        out_specs=[
            pl.BlockSpec(memory_space=VMEM),
            pl.BlockSpec(memory_space=VMEM),
            pl.BlockSpec(memory_space=SMEM),
        ],
        scratch_shapes=[
            pltpu.VMEM(jacobian_blocks.shape, BF16),
            pltpu.SemaphoreType.DMA((rows // chunk,)),
        ],
        cost_estimate=pl.CostEstimate(
            flops=2 * rows * probes * block * block,
            bytes_accessed=rows * (probes * block * 6 + block * block * 10),
            transcendentals=0,
        ),
        compiler_params=LIMIT,
        name="early",
    )(slots, probe_blocks, jacobian_blocks)


def sketch_kernel(inner_count, outer_count, *refs):
    place, users = refs[:2]
    bufs = refs[2 : 2 + inner_count + outer_count]
    base, flipped, high_out, low_out, gram, terms = refs[2 + inner_count + outer_count :]
    inner_slots = bufs[0].shape[0]
    rows, probes, block = base.shape
    for m, buf in enumerate(bufs):
        slots = buf.shape[0]
        if m < inner_count:
            at = (place[0] ^ m) * slots
        else:
            at = inner_count * inner_slots + (place[1] ^ (m - inner_count)) * slots
        for c in range(slots):
            user = users[at + c]
            terms[user] = lax.dot_general(
                buf[c], flipped[user], NN, preferred_element_type=F32
            )

    def one_row(r, total_gram):
        total = base[r] + terms[2 * r] + terms[2 * r + 1]
        high = total.astype(BF16)
        low = (total - high.astype(F32)).astype(BF16)
        high_out[r] = high
        low_out[r] = low
        both = jnp.concatenate([high, low], 0)
        return total_gram + lax.dot_general(both, high, NT, preferred_element_type=F32)

    total_gram = lax.fori_loop(
        0, rows, one_row, jnp.zeros((2 * probes, probes), F32), unroll=8
    )
    cross = total_gram[probes:, :]
    gram[...] = total_gram[:probes, :] + cross + cross.T


def sketched(place, users, inner, outer, base, flipped):
    rows, probes, block = base.shape
    return pl.pallas_call(
        functools.partial(sketch_kernel, len(inner), len(outer)),
        out_shape=[
            jax.ShapeDtypeStruct(base.shape, BF16),
            jax.ShapeDtypeStruct(base.shape, BF16),
            jax.ShapeDtypeStruct((probes, probes), F32),
        ],
        in_specs=[pl.BlockSpec(memory_space=SMEM)] * 2
        + [pl.BlockSpec(memory_space=VMEM)] * (len(inner) + len(outer) + 2),
        out_specs=[pl.BlockSpec(memory_space=VMEM)] * 3,
        scratch_shapes=[pltpu.VMEM((2 * rows, probes, block), F32)],
        cost_estimate=pl.CostEstimate(
            flops=8 * rows * probes * block * block,
            bytes_accessed=rows * (probes * block * 12 + block * block * 4),
            transcendentals=0,
        ),
        compiler_params=LIMIT,
        name="sketch",
    )(place, users, *inner, *outer, base, flipped)


def wide(column, like):
    return jnp.broadcast_to(column, like.shape)


def eliminated(gram):
    size = gram.shape[0]
    row = lax.broadcasted_iota(jnp.int32, (size, size), 0)
    col = lax.broadcasted_iota(jnp.int32, (size, size), 1)
    table = jnp.concatenate([gram, (row == col).astype(F32)], 1)
    tiles = [table[8 * t : 8 * t + 8] for t in range(size // 8)]
    sub = lax.broadcasted_iota(jnp.int32, (8, 2 * size), 0)
    for k in range(0, size, 2):
        t, s = divmod(k, 8)
        here = tiles[t]
        one = wide(here[s : s + 1], here)
        two = wide(here[s + 1 : s + 2], here)
        a = wide(one[:, k : k + 1], here)
        b = wide(one[:, k + 1 : k + 2], here)
        c = wide(two[:, k + 1 : k + 2], here)
        scale = 1.0 / (a * c - b * b)
        a, b, c = a * scale, b * scale, c * scale
        for u in range(t, size // 8):
            if u == t and s == 6:
                continue
            x = wide(tiles[u][:, k : k + 1], here)
            y = wide(tiles[u][:, k + 1 : k + 2], here)
            change = (c * x - b * y) * one + (a * y - b * x) * two
            if u == t:
                change = jnp.where(sub > s + 1, change, 0.0)
            tiles[u] = tiles[u] - change
    table = jnp.concatenate(tiles, 0)
    row = lax.broadcasted_iota(jnp.int32, table.shape, 0)
    col = lax.broadcasted_iota(jnp.int32, table.shape, 1)
    odd = (row & 1) == 1
    above = pltpu.roll(table, 1, 0)
    pivot = jnp.sum(jnp.where(col == row - 1, above, 0.0), 1, keepdims=True)
    below = jnp.sum(jnp.where(col == row - 1, table, 0.0), 1, keepdims=True)
    table = jnp.where(odd, table - wide(below / pivot, table) * above, table)
    diagonal = jnp.sum(jnp.where(col == row, table, 0.0), 1, keepdims=True)
    return table * wide(1.0 / jnp.sqrt(diagonal), table), col >= row


def final_kernel(scale, chunk, count, *refs):
    parts = refs[:count]
    high, low, triangle, basis, high_in, low_in, result, sems = refs[count:]
    rows, probes, block = result.shape
    loads = [
        pltpu.make_async_copy(high, high_in, sems.at[0]),
        pltpu.make_async_copy(low, low_in, sems.at[1]),
    ]
    for load in loads:
        load.start()
    gram = functools.reduce(jnp.add, [p[...] for p in parts]) * scale
    table, upper = eliminated(gram)
    triangle[...] = jnp.where(upper, table, 0.0)[:, :probes]
    inverse = table[:, probes:]
    inverse_high = inverse.astype(BF16)
    inverse_low = (inverse - inverse_high.astype(F32)).astype(BF16)
    left = jnp.concatenate([inverse_high, inverse_high, inverse_low], 1)
    for load in loads:
        load.wait()

    def one_row(r, carry):
        right = jnp.concatenate([high_in[r], low_in[r], high_in[r]], 0)
        result[r] = lax.dot_general(left, right, NN, preferred_element_type=F32)
        return carry

    stores = []
    for q in range(rows // chunk):
        lax.fori_loop(q * chunk, (q + 1) * chunk, one_row, 0, unroll=8)
        part = pl.ds(q * chunk, chunk)
        stores.append(pltpu.make_async_copy(result.at[part], basis.at[part], sems.at[2 + q]))
        stores[-1].start()
    for store in stores:
        store.wait()


def finished(parts, high, low, scale, chunk):
    rows, probes, block = high.shape
    return pl.pallas_call(
        functools.partial(final_kernel, scale, chunk, len(parts)),
        out_shape=[
            jax.ShapeDtypeStruct((probes, probes), F32),
            jax.ShapeDtypeStruct(high.shape, F32),
        ],
        in_specs=[pl.BlockSpec(memory_space=VMEM)] * len(parts)
        + [pl.BlockSpec(memory_space=pl.ANY)] * 2,
        out_specs=[pl.BlockSpec(memory_space=VMEM), pl.BlockSpec(memory_space=pl.ANY)],
        scratch_shapes=[
            pltpu.VMEM(high.shape, BF16),
            pltpu.VMEM(high.shape, BF16),
            pltpu.VMEM(high.shape, F32),
            pltpu.SemaphoreType.DMA((2 + rows // chunk,)),
        ],
        cost_estimate=pl.CostEstimate(
            flops=6 * rows * probes * probes * block,
            bytes_accessed=rows * probes * block * 8,
            transcendentals=0,
        ),
        compiler_params=LIMIT,
        name="final",
    )(*parts, high, low)


def rounds(low_bit, bits):
    while low_bit < bits:
        take = min(2, bits - low_bit)
        yield [m << low_bit for m in range(1, 1 << take)]
        low_bit += take


def shards(jacobian_blocks, probe_blocks, column_slots, want_inner, want_outer):
    row_count, _, block_size, _ = jacobian_blocks.shape
    inner_size = lax.axis_size("dev")
    outer_size = lax.axis_size("grp")
    total_rows = row_count * block_size * inner_size * outer_size
    place = jnp.stack([lax.axis_index("dev"), lax.axis_index("grp")]).astype(jnp.int32)
    if inner_size == 2 * outer_size:
        asks = [paired_asks(want_inner[0], want_outer[0])]
    else:
        asks = [
            lax.all_to_all(want_inner[0], "dev", split_axis=0, concat_axis=0, tiled=True),
            lax.all_to_all(want_outer[0], "grp", split_axis=0, concat_axis=0, tiled=True),
        ]
    inner_masks = sorted(range(inner_size), reverse=True)
    outer_masks = sorted(range(outer_size), reverse=True)
    served = gathered(
        place, asks, want_inner.shape[2], want_outer.shape[2], inner_masks, outer_masks, probe_blocks
    )
    inner = [None] * inner_size
    outer = [None] * outer_size
    for n, m in enumerate(inner_masks):
        inner[m] = swapped(served[n], "dev", m) if m else served[n]
    for n, m in enumerate(outer_masks):
        block = served[inner_size + n]
        outer[m] = swapped(block, "grp", m) if m else block
    base, flipped, users = early_part(column_slots, probe_blocks, jacobian_blocks, 16)
    high, low, part = sketched(place, users, inner, outer, base, flipped)
    part = part + swapped(part, "dev", 1)
    for masks in rounds(1, inner_size.bit_length() - 1):
        part = functools.reduce(jnp.add, [part] + [swapped(part, "dev", m) for m in masks])
    parts = [part]
    for masks in rounds(0, outer_size.bit_length() - 1):
        part = functools.reduce(jnp.add, parts)
        parts = [part] + [swapped(part, "grp", m) for m in masks]
    return tuple(finished(parts, high, low, 1.0 / total_rows, 16))


def solution(mesh):
    return jax.shard_map(
        shards,
        mesh=mesh,
        in_specs=(
            P(("grp", "dev"), None, None, None),
            P(("grp", "dev"), None, None),
            P(("grp", "dev"), None),
            P(("grp", "dev"), None, None),
            P(("grp", "dev"), None, None),
        ),
        out_specs=(P(), P(("grp", "dev"), None, None)),
        check_vma=False,
    )
```
